32 devices in a mesh: dp: 16 (over z, y, core), mp: 2 (over x).
Axes of the slice: x: 2, y: 2, z: 4, core: 2. Of those that a mesh axis runs over, the one named last changes fastest.
Arguments:
- x_in: bfloat16 [32768, 768], P('dp'), may hold values from -6 to 6
- segment_ids: int32 [32, 1024], P('dp'), may hold values from 0 to 15, never falling along the last dimension, each value on 1 to 160 neighbouring positions
- pair_labels: int32 [256], P('dp'), may hold values from 0 to 255
- w_query: float32 [768, 768], P(None, 'mp'), may hold values from -0.21875 to 0.21875
- b_query: float32 [768], P('mp'), may hold values from -3 to 3
- w_key: float32 [768, 768], P(None, 'mp'), may hold values from -0.21875 to 0.21875
- w_value: float32 [768, 768], P(None, 'mp'), may hold values from -0.21875 to 0.21875
- b_value: float32 [768], P('mp'), may hold values from -3 to 3
- w_out: float32 [768, 768], P('mp'), may hold values from -1.75 to 1.75
- b_out: float32 [768], replicated, may hold values from -3 to 3
- gain_attn: float32 [768], replicated, may hold values from 0.1 to 1.9
- shift_attn: float32 [768], replicated, may hold values from -3 to 3
- w_inner: float32 [768, 3072], P(None, 'mp'), may hold values from -0.21875 to 0.21875
- b_inner: float32 [3072], P('mp'), may hold values from -3 to 3
- w_outer: float32 [3072, 768], P('mp'), may hold values from -0.109375 to 0.109375
- b_outer: float32 [768], replicated, may hold values from -3 to 3
- gain_ffn: float32 [768], replicated, may hold values from 0.1 to 1.9
- shift_ffn: float32 [768], replicated, may hold values from -3 to 3
- out_grad: bfloat16 [32768, 768], P(('dp', 'mp')), may hold values from -6 to 6
Outputs:
- scores: float32 [256, 256], P('dp')
- loss: float32 [], replicated
- out_rows: bfloat16 [32768, 768], P(('dp', 'mp'))
- in_grad: float32 [32768, 768], P(('dp', 'mp'))
- grad_w_query: float32 [768, 768], P(None, 'mp')
- grad_b_query: float32 [768], P('mp')
- grad_w_key: float32 [768, 768], P(None, 'mp')
- grad_w_value: float32 [768, 768], P(None, 'mp')
- grad_b_value: float32 [768], P('mp')
- grad_w_out: float32 [768, 768], P('mp')
- grad_b_out: float32 [768], replicated
- grad_gain_attn: float32 [768], replicated
- grad_shift_attn: float32 [768], replicated
- grad_w_inner: float32 [768, 3072], P(None, 'mp')
- grad_b_inner: float32 [3072], P('mp')
- grad_w_outer: float32 [3072, 768], P('mp')
- grad_b_outer: float32 [768], replicated
- grad_gain_ffn: float32 [768], replicated
- grad_shift_ffn: float32 [768], replicated
The draws below stay inside these ranges and needn't reach their ends.
Inputs may be any that keep to these rules, and one draw needn't show every extreme that they name: `segment_ids`: in each row of 1024 positions the segment ids never fall, each of the 16 segments covers 1 to 160 positions and one covers exactly 160; even segments are queries, odd ones passages. `pair_labels`: the index of a query's positive passage among all 256 passages.
All inputs are finite; a program needn't handle non-finite values.
Results may differ from the reference program's by a relative error of at most 0.014.
The reference program's roundings to bfloat16 on the way count: a program that leaves them out, or rounds other values in their place, can miss the bound.
Values may be sent and summed in bfloat16 or wider, within the bound.
No kernel may reach another device: no remote copies, remote signals or barrier semaphores. Data moves between devices by JAX's collectives and lax.ppermute only.
A program may use at most 256 MiB of HBM per device.

```python
import math
import jax
import jax.numpy as jnp
import numpy as np
from jax import lax

D = 768
HEADS = 12
HD = 64
FF = 3072
LEN = 1024
SEGS = 16
MOSTSEG = 160
ROWS = 32
TOKENS = 32768
NQ_ALL = 256
NP_ALL = 256


def touch_ends(entries, own_key, low, high):
    longest = entries.shape.index(max(entries.shape))
    spots = []
    for shift in (0, 1):
        where = [jax.random.randint(jax.random.fold_in(own_key, axis), (), 0, length) for axis, length in enumerate(entries.shape)]
        where[longest] = (where[longest] + shift) % entries.shape[longest]
        spots.append(tuple(where))
    return entries.at[spots[0]].set(low).at[spots[1]].set(high)


def block_scale(stream_key, extent, split, smallest, largest):
    level = 1.0
    for dim, blocks in split:
        heights = jax.random.uniform(jax.random.fold_in(jax.random.fold_in(stream_key, 6), dim), (blocks,), jnp.float32, smallest / len(split), largest / len(split))
        level = level * jnp.repeat(jnp.exp(heights), extent[dim] // blocks).reshape((-1,) + (1,) * (len(extent) - 1 - dim))
    return level


def profile(number_of, total, reach, slope):
    portions = [(1 << 20) // math.isqrt(standing ** slope) + 1 for standing in range(2, number_of + 1)]
    surplus, counts = total - reach - (number_of - 1), [1] * (number_of - 1)
    while surplus > 0:
        candidates = [i for i in range(number_of - 1) if counts[i] < reach]
        pool, budget = sum([portions[i] for i in candidates]), surplus
        for i in candidates:
            addition = min(reach - counts[i], max(1, budget * portions[i] // pool), surplus)
            counts[i] = counts[i] + addition
            surplus = surplus - addition
    return np.array([reach] + counts)


def ragged_sizes(stream_key, count, total, reach, skew):
    if count == 2:
        one = jax.random.randint(stream_key, (), max(1, total - reach), min(reach, total - 1) + 1)
        return jnp.stack([one, total - one])
    tallies = jnp.asarray(profile(count, total, reach, skew), jnp.int32)
    twos = (count - 1) // 2
    giver, sink = tallies[1:1 + 2 * twos:2], tallies[2:2 + 2 * twos:2]
    slack = jnp.minimum(giver - 1, reach - sink)
    moved = jax.random.randint(jax.random.fold_in(stream_key, 1), (twos,), 0, 1 << 20) % (slack + 1)
    tallies = tallies.at[1:1 + 2 * twos:2].set(giver - moved).at[2:2 + 2 * twos:2].set(sink + moved)
    return tallies[jax.random.permutation(jax.random.fold_in(stream_key, 2), count)]


def bell_draw(own_key, dims, deviation, reach, pieces=(), kind=jnp.bfloat16):
    entries = jax.random.normal(own_key, dims, jnp.float32) * deviation
    if len(pieces) > 0:
        entries = block_scale(own_key, dims, pieces, -0.22, 0.18) * entries
    return jnp.clip(entries, min=-reach, max=reach).astype(kind)


def setup_inputs(seed: int = 0) -> dict:
    splits = jax.random.split(jax.random.key(seed), 20)
    return {
        "x_in": bell_draw(splits[0], (TOKENS, D), 1.0, 6.0, ((0, 16),)),
        "segment_ids": jax.vmap(lambda own: jnp.searchsorted(jnp.cumsum(ragged_sizes(own, SEGS, LEN, MOSTSEG, 1)), jnp.arange(LEN), side="right"))(jax.random.split(splits[1], ROWS)).reshape((ROWS, LEN)).astype(jnp.int32),
        "pair_labels": touch_ends(jax.random.randint(splits[2], (NQ_ALL,), 0, NP_ALL), jax.random.fold_in(splits[2], 1), 0, NP_ALL - 1).astype(jnp.int32),
        "w_query": bell_draw(splits[3], (D, D), D ** -0.5, 0.21875, ((1, 2),), jnp.float32),
        "b_query": bell_draw(splits[4], (D,), 0.5, 3.0, ((0, 2),), jnp.float32),
        "w_key": bell_draw(splits[5], (D, D), D ** -0.5, 0.21875, ((1, 2),), jnp.float32),
        "w_value": bell_draw(splits[6], (D, D), D ** -0.5, 0.21875, ((1, 2),), jnp.float32),
        "b_value": bell_draw(splits[7], (D,), 0.5, 3.0, ((0, 2),), jnp.float32),
        "w_out": bell_draw(splits[8], (D, D), (D * SEGS // LEN) ** -0.5, 1.75, ((0, 2),), jnp.float32),
        "b_out": bell_draw(splits[9], (D,), 0.5, 3.0, (), jnp.float32),
        "gain_attn": jnp.clip(1.0 + 0.18 * jax.random.normal(splits[10], (D,), jnp.float32), 0.1, 1.9),
        "shift_attn": bell_draw(splits[11], (D,), 0.5, 3.0, (), jnp.float32),
        "w_inner": bell_draw(splits[12], (D, FF), D ** -0.5, 0.21875, ((1, 2),), jnp.float32),
        "b_inner": bell_draw(splits[13], (FF,), 0.5, 3.0, ((0, 2),), jnp.float32),
        "w_outer": bell_draw(splits[14], (FF, D), FF ** -0.5, 0.109375, ((0, 2),), jnp.float32),
        "b_outer": bell_draw(splits[15], (D,), 0.5, 3.0, (), jnp.float32),
        "gain_ffn": jnp.clip(1.0 + 0.18 * jax.random.normal(splits[16], (D,), jnp.float32), 0.1, 1.9),
        "shift_ffn": bell_draw(splits[17], (D,), 0.5, 3.0, (), jnp.float32),
        "out_grad": bell_draw(splits[18], (TOKENS, D), 1.0, 6.0, ((0, 32),)),
    }


NORM_EPS = 1e-12
MASKED = -1e+30
HIGHEST_PREC = lax.Precision.HIGHEST

@jax.custom_vjp
def low(v):
    return lax.optimization_barrier(v.astype(jnp.bfloat16)).astype(jnp.float32)

@jax.custom_vjp
def low_back(v):
    return v

def low_keep(v):
    return (low(v), None)

def low_pass(kept, grad):
    return (grad,)

def back_keep(v):
    return (v, None)

def back_low(kept, grad):
    return (low(grad),)
low.defvjp(low_keep, low_pass)
low_back.defvjp(back_keep, back_low)

def matmul(left, right):
    return jnp.dot(left, right, precision=HIGHEST_PREC)

def layer_norm(hidden, gain_vec, shift_vec):
    row_mean = lax.optimization_barrier(jnp.mean(hidden, axis=-1, keepdims=True))
    centred = hidden - row_mean
    inv_std = lax.rsqrt(lax.optimization_barrier(jnp.mean(centred * centred, axis=-1, keepdims=True)) + NORM_EPS)
    return centred * inv_std * gain_vec + shift_vec

def layer_row(params, x_row, seg_row):
    w_query, b_query, w_key, w_value, b_value, w_out, b_out, gain_attn, shift_attn, w_inner, b_inner, w_outer, b_outer, gain_ffn, shift_ffn = params
    queries = low(low_back(matmul(x_row, w_query) + b_query)).reshape(LEN, HEADS, HD)
    key_rows = low(low_back(matmul(x_row, w_key))).reshape(LEN, HEADS, HD)
    values = low(low_back(matmul(x_row, w_value) + b_value)).reshape(LEN, HEADS, HD)
    scores = low_back(jnp.einsum('qhd,khd->hqk', queries, key_rows, precision=HIGHEST_PREC) * HD ** (-0.5))
    same_seg = seg_row[:, None] == seg_row[None, :]
    attn_probs = low(jax.nn.softmax(jnp.where(same_seg[None], scores, MASKED), axis=-1))
    mixed_rows = jnp.einsum('hqk,khd->qhd', attn_probs, values, precision=HIGHEST_PREC).reshape(LEN, D)
    attended = low(low_back(mixed_rows))
    first_out = layer_norm(x_row + low_back(matmul(attended, w_out)) + b_out, gain_attn, shift_attn)
    inner_pre = low_back(matmul(low(first_out), w_inner) + b_inner)
    activated = low(jax.nn.gelu(inner_pre, approximate=False))
    return layer_norm(first_out + low_back(matmul(activated, w_outer)) + b_outer, gain_ffn, shift_ffn)

def reference(x_in, segment_ids, pair_labels, w_query, b_query, w_key, w_value, b_value, w_out, b_out, gain_attn, shift_attn, w_inner, b_inner, w_outer, b_outer, gain_ffn, shift_ffn, out_grad):
    params = (w_query, b_query, w_key, w_value, b_value, w_out, b_out, gain_attn, shift_attn, w_inner, b_inner, w_outer, b_outer, gain_ffn, shift_ffn)
    matrix_slots = (0, 2, 3, 5, 9, 11)
    x_rows = x_in.astype(jnp.float32).reshape(ROWS, LEN, D)

    def forward(x_rows, params):
        rounded = tuple((low(member) if position in matrix_slots else member for position, member in enumerate(params)))

        def row_step(carry_sum, row_parts):
            return (carry_sum, jax.checkpoint(layer_row)(rounded, row_parts[0], row_parts[1]))
        unused, outputs = lax.scan(row_step, jnp.zeros((), jnp.float32), (x_rows, segment_ids))
        return outputs
    outputs, pullback = jax.vjp(forward, x_rows, params)
    grad_rows, grad_params = pullback(out_grad.astype(jnp.float32).reshape(ROWS, LEN, D))
    out_low = low(outputs)
    seg_marks = jnp.arange(SEGS, dtype=jnp.int32)
    starts = lax.optimization_barrier(jnp.sum((segment_ids[:, None, :] < seg_marks[None, :, None]).astype(jnp.int32), axis=2))
    heads_cls = out_low[jnp.arange(ROWS, dtype=jnp.int32)[:, None], starts]
    query_vecs = heads_cls[:, 0::2].reshape(-1, D)
    passage_vecs = heads_cls[:, 1::2].reshape(-1, D)
    scores = matmul(query_vecs, passage_vecs.T) * D ** (-0.5)
    picked = jnp.take_along_axis(scores, pair_labels[:, None].astype(jnp.int32), axis=1)[:, 0]
    loss = jnp.mean(jax.nn.logsumexp(scores, axis=1) - picked)
    out_rows = outputs.reshape(TOKENS, D).astype(jnp.bfloat16)
    in_grad = grad_rows.reshape(TOKENS, D)
    return (scores, loss, out_rows, in_grad, grad_params[0], grad_params[1], grad_params[2], grad_params[3], grad_params[4], grad_params[5], grad_params[6], grad_params[7], grad_params[8], grad_params[9], grad_params[10], grad_params[11], grad_params[12], grad_params[13], grad_params[14])
```

```python
import jax
import jax.numpy as jnp
from jax import lax
from jax.experimental import pallas as pl
from jax.experimental.pallas import tpu as pltpu
from jax.sharding import PartitionSpec as P

HD = 64
SEGS = 16
MOST_SEG = 160
Q_BLOCK = 128
K_WINDOW = 512
K_LEAD = 192

NORM_EPS = 1e-12
MASKED = -1e30
HALF_ROOT = 0.7071067811865476
INV_ROOT_TAU = 0.3989422804014327


def layer_norm(hidden, gain_vec, shift_vec):
    row_mean = jnp.mean(hidden, axis=-1, keepdims=True)
    centred = hidden - row_mean
    inv_std = lax.rsqrt(jnp.mean(centred * centred, axis=-1, keepdims=True) + NORM_EPS)
    normed = centred * inv_std
    return (normed * gain_vec + shift_vec, normed, inv_std)


def norm_back(grad_out, normed, inv_std, gain_vec):
    scaled = grad_out * gain_vec
    grad_in = inv_std * (
        scaled
        - jnp.mean(scaled, axis=-1, keepdims=True)
        - normed * jnp.mean(scaled * normed, axis=-1, keepdims=True)
    )
    return (grad_in, jnp.sum(grad_out * normed, axis=0), jnp.sum(grad_out, axis=0))


def dot_rows(left, right):
    return jnp.dot(left, right, preferred_element_type=jnp.float32)


def contract_rows(left, right):
    return lax.dot_general(
        left, right, (((0,), (0,)), ((), ())), preferred_element_type=jnp.float32
    )


def times_trans(left, right):
    return lax.dot_general(
        left, right, (((1,), (1,)), ((), ())), preferred_element_type=jnp.float32
    )


def window_start(block, seq_len):
    return pl.multiple_of(jnp.clip(block * Q_BLOCK - K_LEAD, 0, seq_len - K_WINDOW), 64)


def head_masks(scale):
    lane = lax.broadcasted_iota(jnp.int32, (1, 2 * HD), 1)
    low = jnp.where(lane < HD, scale, 0.0).astype(jnp.bfloat16)
    high = jnp.where(lane < HD, 0.0, scale).astype(jnp.bfloat16)
    return low, high


def stack_heads(rows, masks):
    return jnp.concatenate([rows * masks[0], rows * masks[1]], axis=0)


def unstack_trans(both):
    row = lax.broadcasted_iota(jnp.int32, (2 * HD, Q_BLOCK), 0)
    return jnp.where(row < HD, both[:, :Q_BLOCK], both[:, Q_BLOCK:]).T


def seg_bias(seg_cols, seg_line):
    bias = jnp.where(seg_cols == seg_line, 0.0, MASKED)
    return jnp.concatenate([bias, bias], axis=1)


def attend_kernel(q_ref, k_ref, v_ref, line_ref, cols_ref, o_ref, lse_ref):
    seq_len = q_ref.shape[0]
    masks = head_masks(HD ** (-0.5))

    def one_block(block, carry):
        start = window_start(block, seq_len)
        here = pl.ds(pl.multiple_of(block * Q_BLOCK, Q_BLOCK), Q_BLOCK)
        there = pl.ds(start, K_WINDOW)
        queries = stack_heads(q_ref[here, :], masks)
        bias = seg_bias(cols_ref[there, :], line_ref[0, pl.ds(block, 1), :])
        scores = times_trans(k_ref[there, :], queries) + bias
        top = jnp.max(scores, axis=0, keepdims=True)
        raised = jnp.exp(scores - top)
        total = jnp.sum(raised, axis=0, keepdims=True)
        probs = (raised * (1.0 / total)).astype(jnp.bfloat16)
        mixed = contract_rows(v_ref[there, :], probs)
        o_ref[here, :] = unstack_trans(mixed).astype(jnp.bfloat16)
        lse_ref[0, 0, pl.ds(block, 1), :] = top + jnp.log(total)
        return carry

    lax.fori_loop(0, seq_len // Q_BLOCK, one_block, 0)


def attend(qkv, seg_lines, seg_cols):
    tokens, width = qkv.shape
    rows, blocks, _ = seg_lines.shape
    seq_len = tokens // rows
    pairs = width // 3 // (2 * HD)

    def part(which):
        return pl.BlockSpec((seq_len, 2 * HD), lambda r, p: (r, which * pairs + p))

    return pl.pallas_call(
        attend_kernel,
        grid=(rows, pairs),
        in_specs=[
            part(0),
            part(1),
            part(2),
            pl.BlockSpec((1, blocks, Q_BLOCK), lambda r, p: (r, 0, 0)),
            pl.BlockSpec((seq_len, Q_BLOCK), lambda r, p: (r, 0)),
        ],
        out_specs=[
            pl.BlockSpec((seq_len, 2 * HD), lambda r, p: (r, p)),
            pl.BlockSpec((1, 1, blocks, 2 * Q_BLOCK), lambda r, p: (r, p, 0, 0)),
        ],
        out_shape=[
            jax.ShapeDtypeStruct((tokens, width // 3), jnp.bfloat16),
            jax.ShapeDtypeStruct((rows, pairs, blocks, 2 * Q_BLOCK), jnp.float32),
        ],
        name="attend",
    )(qkv, qkv, qkv, seg_lines, seg_cols)


def attend_back_kernel(
    q_ref, k_ref, v_ref, do_ref, lse_ref, line_ref, cols_ref, out_ref, dk_ref, dv_ref
):
    seq_len = q_ref.shape[0]
    pair = pl.program_id(1)
    third = out_ref.shape[1] // 3
    scaled_masks = head_masks(HD ** (-0.5))
    plain_masks = head_masks(1.0)
    dk_ref[...] = jnp.zeros_like(dk_ref)
    dv_ref[...] = jnp.zeros_like(dv_ref)
    lanes = pl.multiple_of(pair * 2 * HD, 2 * HD)

    def one_block(block, carry):
        start = window_start(block, seq_len)
        here = pl.ds(pl.multiple_of(block * Q_BLOCK, Q_BLOCK), Q_BLOCK)
        there = pl.ds(start, K_WINDOW)
        queries = stack_heads(q_ref[here, :], scaled_masks)
        grads = stack_heads(do_ref[here, :], plain_masks)
        keys = k_ref[there, :]
        bias = seg_bias(cols_ref[there, :], line_ref[0, pl.ds(block, 1), :])
        probs = jnp.exp(times_trans(keys, queries) + bias - lse_ref[0, 0, pl.ds(block, 1), :])
        grad_probs = times_trans(v_ref[there, :], grads)
        centre = jnp.sum(probs * grad_probs, axis=0, keepdims=True)
        grad_scores = (probs * (grad_probs - centre)).astype(jnp.bfloat16)
        dv_ref[there, :] += dot_rows(probs.astype(jnp.bfloat16), grads)
        dk_ref[there, :] += dot_rows(grad_scores, queries)
        grad_q = unstack_trans(contract_rows(keys, grad_scores)) * HD ** (-0.5)
        out_ref[here, pl.ds(lanes, 2 * HD)] = grad_q.astype(jnp.bfloat16)
        return carry

    lax.fori_loop(0, seq_len // Q_BLOCK, one_block, 0)
    out_ref[:, pl.ds(pl.multiple_of(third + lanes, 2 * HD), 2 * HD)] = dk_ref[...].astype(
        jnp.bfloat16
    )
    out_ref[:, pl.ds(pl.multiple_of(2 * third + lanes, 2 * HD), 2 * HD)] = dv_ref[...].astype(
        jnp.bfloat16
    )


def attend_back(qkv, grad_out, lse, seg_lines, seg_cols):
    tokens, width = qkv.shape
    rows, blocks, _ = seg_lines.shape
    seq_len = tokens // rows
    pairs = width // 3 // (2 * HD)

    def part(which):
        return pl.BlockSpec((seq_len, 2 * HD), lambda r, p: (r, which * pairs + p))

    return pl.pallas_call(
        attend_back_kernel,
        grid=(rows, pairs),
        in_specs=[
            part(0),
            part(1),
            part(2),
            part(0),
            pl.BlockSpec((1, 1, blocks, 2 * Q_BLOCK), lambda r, p: (r, p, 0, 0)),
            pl.BlockSpec((1, blocks, Q_BLOCK), lambda r, p: (r, 0, 0)),
            pl.BlockSpec((seq_len, Q_BLOCK), lambda r, p: (r, 0)),
        ],
        out_specs=pl.BlockSpec((seq_len, width), lambda r, p: (r, 0)),
        out_shape=jax.ShapeDtypeStruct((tokens, width), jnp.bfloat16),
        scratch_shapes=[pltpu.VMEM((seq_len, 2 * HD), jnp.float32)] * 2,
        name="attend_back",
    )(qkv, qkv, qkv, grad_out, lse, seg_lines, seg_cols)


def swap_mp(value):
    count = lax.axis_size("mp")
    return lax.ppermute(value, "mp", [(i, i ^ 1) for i in range(count)])


def swap_dp(value, bit):
    count = lax.axis_size("dp")
    return lax.ppermute(value, "dp", [(i, i ^ (1 << bit)) for i in range(count)])


def dp_bits():
    return (lax.axis_size("dp") - 1).bit_length()


def bit_of(bit):
    return (lax.axis_index("dp") >> bit) & 1


def half_of(value, which):
    size = value.shape[0] // 2
    return lax.dynamic_slice_in_dim(value, which * size, size, 0)


def join_halves(own, other, own_is_high):
    first = jnp.where(own_is_high == 0, own, other)
    second = jnp.where(own_is_high == 0, other, own)
    return jnp.concatenate([first, second], axis=0)


def fetch_other(own):
    side = bit_of(0)
    mine = swap_mp(half_of(own, side))
    return join_halves(mine, swap_dp(mine, 0), side)


def reduce_weight(own, other):
    side = bit_of(0)
    got_other = swap_dp(half_of(other, 1 - side), 0)
    part_other = (
        half_of(other, side).astype(jnp.float32) + got_other.astype(jnp.float32)
    ).astype(jnp.bfloat16)
    got_own = swap_dp(half_of(own, 1 - side), 0)
    crossed = swap_mp(part_other)
    part = (
        half_of(own, side).astype(jnp.float32)
        + got_own.astype(jnp.float32)
        + crossed.astype(jnp.float32)
    ).astype(jnp.bfloat16)
    for bit in range(1, dp_bits()):
        side = bit_of(bit)
        got = swap_dp(half_of(part, 1 - side), bit)
        part = (half_of(part, side).astype(jnp.float32) + got.astype(jnp.float32)).astype(
            jnp.bfloat16
        )
    for bit in reversed(range(dp_bits())):
        part = join_halves(part, swap_dp(part, bit), bit_of(bit))
    return part.astype(jnp.float32)


def reduce_small(own, other, shared):
    width = own.shape[0]
    crossed = swap_mp(jnp.concatenate([other, shared]))
    total = jnp.concatenate([own, shared]) + crossed
    for bit in range(dp_bits()):
        total = total + swap_dp(total, bit)
    return total[:width], total[width:]


def gather_rows(part):
    part = join_halves(part, swap_mp(part), lax.axis_index("mp"))
    for bit in range(dp_bits()):
        part = join_halves(part, swap_dp(part, bit), bit_of(bit))
    return part


def body(
    x_in,
    segment_ids,
    pair_labels,
    w_query,
    b_query,
    w_key,
    w_value,
    b_value,
    w_out,
    b_out,
    gain_attn,
    shift_attn,
    w_inner,
    b_inner,
    w_outer,
    b_outer,
    gain_ffn,
    shift_ffn,
    out_grad,
):
    rows_here, seq_len = segment_ids.shape
    mp_count = lax.axis_size("mp")
    mp_index = lax.axis_index("mp")
    model_width = x_in.shape[1]
    rows = rows_here // mp_count
    tokens = rows * seq_len
    blocks = seq_len // Q_BLOCK
    x_low = lax.dynamic_slice_in_dim(x_in, mp_index * tokens, tokens, 0)
    segs = lax.dynamic_slice_in_dim(segment_ids, mp_index * rows, rows, 0)
    seg_lines = segs.reshape(rows, blocks, Q_BLOCK)
    seg_cols = jnp.broadcast_to(segs.reshape(tokens, 1), (tokens, Q_BLOCK))

    heads_width = w_query.shape[1]
    qkv_own = jnp.concatenate([w_query, w_key, w_value], axis=1).astype(jnp.bfloat16)
    out_own = w_out.astype(jnp.bfloat16)
    inner_own = w_inner.astype(jnp.bfloat16)
    outer_own = w_outer.astype(jnp.bfloat16)
    bias_qkv_own = jnp.concatenate([b_query, jnp.zeros_like(b_query), b_value])
    biases_other = swap_mp(jnp.concatenate([bias_qkv_own, b_inner]))
    bias_qkv_other = biases_other[: 3 * heads_width]
    b_inner_other = biases_other[3 * heads_width :]
    qkv_other = fetch_other(qkv_own)
    out_other = fetch_other(out_own)
    inner_other = fetch_other(inner_own)
    outer_other = fetch_other(outer_own)

    mixed = []
    for weight, bias in ((qkv_own, bias_qkv_own), (qkv_other, bias_qkv_other)):
        projected = (dot_rows(x_low, weight) + bias).astype(jnp.bfloat16)
        attended, lse = attend(projected, seg_lines, seg_cols)
        mixed.append((projected, attended, lse))
    (proj_own, att_own, lse_own), (proj_other, att_other, lse_other) = mixed
    hidden = (
        x_low.astype(jnp.float32)
        + (dot_rows(att_own, out_own) + dot_rows(att_other, out_other))
        + b_out
    )
    first_out, normed_a, inv_a = layer_norm(hidden, gain_attn, shift_attn)
    first_low = first_out.astype(jnp.bfloat16)
    inner_pre = []
    activated = []
    for weight, bias in ((inner_own, b_inner), (inner_other, b_inner_other)):
        pre = dot_rows(first_low, weight) + bias
        inner_pre.append(pre)
        activated.append(jax.nn.gelu(pre, approximate=False).astype(jnp.bfloat16))
    hidden = (
        first_out
        + (dot_rows(activated[0], outer_own) + dot_rows(activated[1], outer_other))
        + b_outer
    )
    output, normed_f, inv_f = layer_norm(hidden, gain_ffn, shift_ffn)
    out_rows = output.astype(jnp.bfloat16)

    seg_marks = jnp.arange(SEGS, dtype=jnp.int32)
    starts = jnp.sum((segs[:, None, :] < seg_marks[None, :, None]).astype(jnp.int32), axis=2)
    places = starts + (jnp.arange(rows, dtype=jnp.int32) * seq_len)[:, None]
    picker = (
        places.reshape(-1)[:, None] == jnp.arange(tokens, dtype=jnp.int32)[None, :]
    ).astype(jnp.bfloat16)
    heads_cls = (
        dot_rows(picker, out_rows)
        .astype(jnp.bfloat16)
        .reshape(rows, SEGS // 2, 2, model_width)
    )
    query_vecs = heads_cls[:, :, 0].reshape(-1, model_width)
    passages = gather_rows(heads_cls[:, :, 1].reshape(-1, model_width))
    own_scores = times_trans(query_vecs, passages) * model_width ** (-0.5)
    own_queries = own_scores.shape[0]
    score_top = jnp.max(own_scores, axis=1)
    score_lse = score_top + jnp.log(jnp.sum(jnp.exp(own_scores - score_top[:, None]), axis=1))
    labels = lax.dynamic_slice_in_dim(pair_labels, mp_index * own_queries, own_queries, 0)
    label_hits = labels[:, None] == jnp.arange(own_scores.shape[1], dtype=jnp.int32)[None, :]
    picked = jnp.sum(jnp.where(label_hits, own_scores, 0.0), axis=1)
    loss_part = jnp.sum(score_lse - picked)
    scores = join_halves(own_scores, swap_mp(own_scores), mp_index)

    grad_h2, grad_gain_ffn, grad_shift_ffn = norm_back(
        out_grad.astype(jnp.float32), normed_f, inv_f, gain_ffn
    )
    grad_b_outer = jnp.sum(grad_h2, axis=0)
    grad_h2_low = grad_h2.astype(jnp.bfloat16)
    grad_w_outer = [contract_rows(act, grad_h2_low).astype(jnp.bfloat16) for act in activated]
    sum_w_outer = reduce_weight(*grad_w_outer)
    grad_first = grad_h2
    grad_b_inner = []
    grad_w_inner = []
    for pre, inner, outer in (
        (inner_pre[0], inner_own, outer_own),
        (inner_pre[1], inner_other, outer_other),
    ):
        slope = 0.5 * (1.0 + lax.erf(pre * HALF_ROOT)) + pre * INV_ROOT_TAU * jnp.exp(
            -0.5 * pre * pre
        )
        grad_inner = (times_trans(grad_h2_low, outer) * slope).astype(jnp.bfloat16)
        grad_b_inner.append(jnp.sum(grad_inner.astype(jnp.float32), axis=0))
        grad_w_inner.append(contract_rows(first_low, grad_inner).astype(jnp.bfloat16))
        grad_first = grad_first + times_trans(grad_inner, inner)
    sum_w_inner = reduce_weight(*grad_w_inner)

    grad_h1, grad_gain_attn, grad_shift_attn = norm_back(grad_first, normed_a, inv_a, gain_attn)
    grad_b_out = jnp.sum(grad_h1, axis=0)
    grad_h1_low = grad_h1.astype(jnp.bfloat16)
    sum_w_out = reduce_weight(
        contract_rows(att_own, grad_h1_low).astype(jnp.bfloat16),
        contract_rows(att_other, grad_h1_low).astype(jnp.bfloat16),
    )
    in_grad = grad_h1
    grad_w_qkv = []
    grad_b_qkv = []
    for projected, lse, out_w, qkv_w in (
        (proj_other, lse_other, out_other, qkv_other),
        (proj_own, lse_own, out_own, qkv_own),
    ):
        grad_attended = times_trans(grad_h1_low, out_w).astype(jnp.bfloat16)
        grad_qkv = attend_back(projected, grad_attended, lse, seg_lines, seg_cols)
        grad_b_qkv.append(jnp.sum(grad_qkv.astype(jnp.float32), axis=0))
        grad_w_qkv.append(contract_rows(x_low, grad_qkv).astype(jnp.bfloat16))
        in_grad = in_grad + times_trans(grad_qkv, qkv_w)
    sum_w_qkv = reduce_weight(grad_w_qkv[1], grad_w_qkv[0])

    own_sums, shared_sums = reduce_small(
        jnp.concatenate([grad_b_qkv[1], grad_b_inner[0]]),
        jnp.concatenate([grad_b_qkv[0], grad_b_inner[1]]),
        jnp.concatenate(
            [
                grad_b_out,
                grad_gain_attn,
                grad_shift_attn,
                grad_b_outer,
                grad_gain_ffn,
                grad_shift_ffn,
                jnp.full((128,), loss_part),
            ]
        ),
    )
    (
        grad_b_out,
        grad_gain_attn,
        grad_shift_attn,
        grad_b_outer,
        grad_gain_ffn,
        grad_shift_ffn,
    ) = jnp.split(shared_sums[: 6 * model_width], 6)
    query_total = own_queries * mp_count * lax.axis_size("dp")
    loss = shared_sums[6 * model_width] / query_total
    return (
        scores,
        loss,
        out_rows,
        in_grad,
        sum_w_qkv[:, :heads_width],
        own_sums[:heads_width],
        sum_w_qkv[:, heads_width : 2 * heads_width],
        sum_w_qkv[:, 2 * heads_width :],
        own_sums[2 * heads_width : 3 * heads_width],
        sum_w_out,
        grad_b_out,
        grad_gain_attn,
        grad_shift_attn,
        sum_w_inner,
        own_sums[3 * heads_width :],
        sum_w_outer,
        grad_b_outer,
        grad_gain_ffn,
        grad_shift_ffn,
    )


def solution(mesh):
    return jax.shard_map(
        body,
        mesh=mesh,
        in_specs=(
            P("dp", None),
            P("dp", None),
            P("dp"),
            P(None, "mp"),
            P("mp"),
            P(None, "mp"),
            P(None, "mp"),
            P("mp"),
            P("mp", None),
            P(),
            P(),
            P(),
            P(None, "mp"),
            P("mp"),
            P("mp", None),
            P(),
            P(),
            P(),
            P(("dp", "mp"), None),
        ),
        out_specs=(
            P("dp", None),
            P(),
            P(("dp", "mp"), None),
            P(("dp", "mp"), None),
            P(None, "mp"),
            P("mp"),
            P(None, "mp"),
            P(None, "mp"),
            P("mp"),
            P("mp", None),
            P(),
            P(),
            P(),
            P(None, "mp"),
            P("mp"),
            P("mp", None),
            P(),
            P(),
            P(),
        ),
        check_vma=False,
    )
```
